512 devices in a mesh: aa: 16 (over x, y_lo, core), ba: 32 (over y_hi, z).
Axes of the slice: x: 4, y: 4 (y_hi: 2, y_lo: 2; y = y_hi * 2 + y_lo), z: 16, core: 2. Of those that a mesh axis runs over, the one named last changes fastest.
Arguments:
- coefficients: float32 [12288, 12288], P('aa', 'ba'), may hold values from -6 to 6
- tile_values: bfloat16 [16, 3, 768, 768], P('aa'), may hold values from -0.125 to 0.125
- tile_cols: int32 [16, 3], P('aa'), may hold values from 0 to 15, as said below
- alpha_energy: float32 [12288], P('aa'), may hold values from -1 to 1
- beta_energy: float32 [12288], P('ba'), may hold values from -1 to 1
Outputs:
- sigma: float32 [12288, 12288], P('aa', 'ba')
The draws below stay inside these ranges and needn't reach their ends.
Inputs may be any that keep to these rules, and one draw needn't show every extreme that they name: Row r of tile_cols holds r - 1, r and r + 1 taken modulo 16, each once, in some order.
All inputs are finite; a program needn't handle non-finite values.
Results may differ from the reference program's by a relative error of at most 0.0027.
Values may be sent and summed in bfloat16 or wider, within the bound.
No kernel may reach another device: no remote copies, remote signals or barrier semaphores. Data moves between devices by JAX's collectives and lax.ppermute only.
A program may use at most 64 MiB of HBM per device.

```python
from functools import partial
import jax
import jax.numpy as jnp
from jax import lax

TILE = 768
SLOTS = 3
NBLK = 16
NSTR = 12288


def draw_tile_cols(key, part):
    rows_ids = jnp.arange(NBLK, dtype=jnp.int32)
    scores = jax.random.randint(key, (NBLK, 3), 0, 1000, dtype=jnp.int32) * 3 + jnp.arange(3, dtype=jnp.int32)[None, :]
    order = jnp.argsort(scores, axis=1, stable=True).astype(jnp.int32)
    offsets = order - 1
    return ((rows_ids[:, None] + offsets + NBLK) % NBLK).astype(jnp.int32)


def block_levels(stream_key, extent, split, least, top_value):
    loudness, own = 1.0, jax.random.fold_in(stream_key, 6)
    for position, shards_of in split:
        steps = jnp.exp(jax.random.uniform(jax.random.fold_in(own, position), (shards_of,), jnp.float32, least / len(split), top_value / len(split)))
        loudness = loudness * jnp.repeat(steps, extent[position] // shards_of).reshape([-1 if axis == position else 1 for axis in range(len(extent))])
    return loudness


def centred(stream_key, shape, scale, limit, pieces=(), held_as=jnp.bfloat16):
    entries = jax.random.normal(stream_key, shape, jnp.float32) * scale
    if len(pieces) > 0:
        entries = block_levels(stream_key, shape, pieces, -0.22, 0.18) * entries
    return jnp.clip(entries, min=-limit, max=limit).astype(held_as)


def setup_inputs(seed: int = 0) -> dict:
    arg_keys = jax.random.split(jax.random.key(seed), 6)
    return {
        "coefficients": centred(arg_keys[0], (NSTR, NSTR), 1.0, 6.0, ((0, 16), (1, 32)), jnp.float32),
        "tile_values": centred(arg_keys[1], (NBLK, SLOTS, TILE, TILE), (3 * TILE) ** -0.5, 0.125, ((0, 16),)),
        "tile_cols": draw_tile_cols(jax.random.fold_in(arg_keys[5], 71), 0),
        "alpha_energy": jnp.clip(jax.random.uniform(arg_keys[3], (NSTR,), jnp.float32, -1.0, 1.0) * block_levels(arg_keys[3], (NSTR,), ((0, 16),), -0.4, 0.0), -1.0, 1.0),
        "beta_energy": jnp.clip(jax.random.uniform(arg_keys[4], (NSTR,), jnp.float32, -1.0, 1.0) * block_levels(arg_keys[4], (NSTR,), ((0, 32),), -0.4, 0.0), -1.0, 1.0),
    }


def block_rows(source, entry):
    tile_group, col_ids = entry
    summed = jnp.zeros((TILE, NSTR), jnp.float32)
    for slot in range(SLOTS):
        picked = lax.dynamic_index_in_dim(source, col_ids[slot].astype(jnp.int32), 0, keepdims=False)
        summed = summed + jnp.dot(tile_group[slot].astype(jnp.float32), picked, precision=lax.Precision.HIGHEST)
    return summed


def reference(coefficients, tile_values, tile_cols, alpha_energy, beta_energy):
    coeff_low = coefficients.astype(jnp.bfloat16).astype(jnp.float32)
    blocks = coeff_low.reshape(NBLK, TILE, NSTR)
    alpha_term = lax.map(partial(block_rows, blocks), (tile_values, tile_cols)).reshape(NSTR, NSTR)
    flipped = coeff_low.T.reshape(NBLK, TILE, NSTR)
    beta_flip = lax.map(partial(block_rows, flipped), (tile_values, tile_cols)).reshape(NSTR, NSTR)
    energy = alpha_energy[:, None] + beta_energy[None, :]
    return alpha_term + beta_flip.T + energy * coefficients
```

```python
import jax
import jax.numpy as jnp
from jax import lax
from jax.sharding import PartitionSpec as P

BOTH = ("aa", "ba")


def permuted(value, send_to, rows, cols):
    pairs = []
    for a in range(rows):
        for b in range(cols):
            ta, tb = send_to(a, b)
            pairs.append((a * cols + b, ta * cols + tb))
    return lax.ppermute(value, BOTH, pairs)


def scatter_source(b_target, a_target):
    row, half = b_target // 2, b_target % 2
    upper, depth = b_target // 16, b_target % 16
    x, y, core = a_target // 4, (a_target // 2) % 2, a_target % 2
    row_y = (row // 2) % 2
    source_upper = upper if row_y == y else 1 - upper
    distance = x * 2 + core
    source_depth = (depth - distance) % 16 if half == 0 else (depth + distance) % 16
    return source_upper * 16 + source_depth


def body(coefficients, tile_values, tile_cols, alpha_energy, beta_energy):
    rows, cols = lax.axis_size("aa"), lax.axis_size("ba")
    tile = tile_values.shape[2]
    chunk = tile // 2
    piece = tile // rows
    a, b = lax.axis_index("aa"), lax.axis_index("ba")

    table = [[0] * cols for _ in range(rows)]
    route = {}
    for ta in range(rows):
        for tb in range(cols):
            sa, sb = tb // 2, scatter_source(tb, ta)
            table[sa][sb] = ta * 2 + tb % 2
            route[(sa, sb)] = (ta, tb)
    served = jnp.asarray(table, jnp.int32)[a, b]
    half = served % 2
    near_block = jnp.where(half == 0, (a + rows - 1) % rows, (a + 1) % rows)
    slots = jnp.arange(3, dtype=jnp.int32)
    near_slot = jnp.sum(jnp.where(tile_cols[0] == near_block, slots, 0))
    own_slot = jnp.sum(jnp.where(tile_cols[0] == a, slots, 0))
    above_slot = jnp.sum(jnp.where(tile_cols[0] == (a + 1) % rows, slots, 0))
    below_slot = jnp.sum(jnp.where(tile_cols[0] == (a + rows - 1) % rows, slots, 0))
    target = served // 2
    tx, ty, tc = target // 4, (target // 2) % 2, target % 2
    order = tc * 8 + tx * 2 + ty
    row_start = (order * piece + half * chunk) % tile

    def cut(slot, col):
        return lax.dynamic_slice(tile_values, (0, slot, row_start, col), (1, 1, piece, chunk))[0, 0]

    parts = jnp.stack(
        [cut(near_slot, (1 - half) * chunk), cut(near_slot, half * chunk), cut(own_slot, half * chunk)], axis=0
    )
    got = permuted(parts, lambda i, j: route[(i, j)], rows, cols)

    low = coefficients.astype(jnp.bfloat16)
    near = lax.ppermute(low, "ba", [(j, (j + 1) % cols if j % 2 else (j - 1) % cols) for j in range(cols)])
    far = lax.ppermute(low, "ba", [(j, (j - 2) % cols if j % 2 else (j + 2) % cols) for j in range(cols)])
    from_above = lax.ppermute(low, "aa", [(i, (i - 1) % rows) for i in range(rows)])
    from_below = lax.ppermute(low, "aa", [(i, (i + 1) % rows) for i in range(rows)])

    my_x, my_y, my_core = a // 4, (a // 2) % 2, a % 2
    other_y = lax.ppermute(got, "aa", [(i, i ^ 2) for i in range(rows)])
    pair = jnp.zeros((3, 2, piece, chunk), jnp.bfloat16)
    pair = lax.dynamic_update_slice(pair, got[:, None], (0, my_y, 0, 0))
    pair = lax.dynamic_update_slice(pair, other_y[:, None], (0, 1 - my_y, 0, 0))
    quad = jnp.zeros((3, 4, 2, piece, chunk), jnp.bfloat16)
    quad = lax.dynamic_update_slice(quad, pair[:, None], (0, my_x, 0, 0, 0))
    for step in (1, 2, 3):
        moved = lax.ppermute(pair, "aa", [(i, (i - 4 * step) % rows) for i in range(rows)])
        quad = lax.dynamic_update_slice(quad, moved[:, None], (0, (my_x + step) % 4, 0, 0, 0))
    quad = quad.reshape(3, 8 * piece, chunk)
    other_core = lax.ppermute(quad, "aa", [(i, i ^ 1) for i in range(rows)])
    weight = jnp.zeros((3, 2, 8 * piece, chunk), jnp.bfloat16)
    weight = lax.dynamic_update_slice(weight, quad[:, None], (0, my_core, 0, 0))
    weight = lax.dynamic_update_slice(weight, other_core[:, None], (0, 1 - my_core, 0, 0))
    weight = weight.reshape(3, tile, chunk)

    def times(left, right):
        return lax.dot_general(left, right, (((1,), (1,)), ((), ())), preferred_element_type=jnp.float32)

    def beta_part(rows_of):
        total = times(near, weight[0, rows_of])
        total = total + times(far, weight[1, rows_of])
        return total + times(low, weight[2, rows_of])

    sent = beta_part(slice(chunk, None)).astype(jnp.bfloat16)
    received = lax.ppermute(sent, "ba", [(j, j ^ 1) for j in range(cols)])
    kept = beta_part(slice(0, chunk))

    def tile_of(slot):
        return lax.dynamic_slice(tile_values, (0, slot, 0, 0), (1, 1, tile, tile))[0, 0]

    alpha = jnp.dot(tile_of(own_slot), low, preferred_element_type=jnp.float32)
    alpha = alpha + jnp.dot(tile_of(above_slot), from_above, preferred_element_type=jnp.float32)
    alpha = alpha + jnp.dot(tile_of(below_slot), from_below, preferred_element_type=jnp.float32)
    energy = alpha_energy[:, None] + beta_energy[None, :]
    return alpha + energy * coefficients + kept + received.astype(jnp.float32)


def solution(mesh):
    in_specs = (P("aa", "ba"), P("aa", None, None, None), P("aa", None), P("aa"), P("ba"))
    out_specs = P("aa", "ba")
    return jax.shard_map(body, mesh=mesh, in_specs=in_specs, out_specs=out_specs, check_vma=False)
```

```python
import jax
import jax.numpy as jnp
from jax import lax
from jax.experimental import pallas as pl
from jax.experimental.pallas import tpu as pltpu
from jax.sharding import PartitionSpec as P


BOTH = ("aa", "ba")


def served_by(row, col):
    upper, depth = col // 16, col % 16
    ahead = (depth - 2 * row) % 16
    is_right = (ahead >= 1) * (ahead <= 8)
    distance = is_right * (ahead - 1) + (1 - is_right) * ((16 - ahead) % 16)
    x, core = distance // 2, distance % 2
    y = ((row // 2) + upper + row // 8) % 2
    return x * 4 + y * 2 + core, 2 * row + is_right


def pick_kernel(cols_ref, tiles_ref, out_ref, sems, *, rows, piece, chunk):
    row = lax.axis_index("aa")
    col = lax.axis_index("ba")
    upper, depth = lax.div(col, 16), lax.rem(col, 16)
    ahead = lax.rem(depth - lax.rem(2 * row, 16) + 16, 16)
    is_right = jnp.where((ahead >= 1) & (ahead <= 8), 1, 0)
    distance = jnp.where(is_right == 1, ahead - 1, lax.rem(16 - ahead, 16))
    x, core = lax.div(distance, 2), lax.rem(distance, 2)
    y = lax.rem(lax.div(row, 2) + upper + lax.div(row, 8), 2)
    order = core * 8 + x * 2 + y
    start = lax.rem(order * piece + is_right * chunk, 2 * chunk)
    wanted = lax.rem(row + jnp.where(is_right == 1, 1, rows - 1), rows)
    near_slot = jnp.where(cols_ref[0, 1] == wanted, 1, jnp.where(cols_ref[0, 2] == wanted, 2, 0))
    own_slot = jnp.where(cols_ref[0, 1] == row, 1, jnp.where(cols_ref[0, 2] == row, 2, 0))

    def copy(index, slot, side):
        return pltpu.make_async_copy(
            tiles_ref.at[0, slot, pl.ds(pl.multiple_of(start, 16), piece), pl.ds(pl.multiple_of(side * chunk, 128), chunk)],
            out_ref.at[index],
            sems.at[index],
        )

    copies = [copy(0, near_slot, 1 - is_right), copy(1, near_slot, is_right), copy(2, own_slot, is_right)]
    for each in copies:
        each.start()
    for each in copies:
        each.wait()


def pick(tile_cols, tile_values, rows):
    tile = tile_values.shape[2]
    piece, chunk = tile // rows, tile // 2

    def kernel(cols_ref, tiles_ref, out_ref, sems):
        pick_kernel(cols_ref, tiles_ref, out_ref, sems, rows=rows, piece=piece, chunk=chunk)

    return pl.pallas_call(
        kernel,
        out_shape=jax.ShapeDtypeStruct((3, piece, chunk), jnp.bfloat16),
        in_specs=[pl.BlockSpec(memory_space=pltpu.SMEM), pl.BlockSpec(memory_space=pl.ANY)],
        out_specs=pl.BlockSpec(memory_space=pl.ANY),
        scratch_shapes=[pltpu.SemaphoreType.DMA((3,))],
        name="pick",
    )(tile_cols, tile_values)


def body(coefficients, tile_values, tile_cols, alpha_energy, beta_energy):
    rows, cols = lax.axis_size("aa"), lax.axis_size("ba")
    tile = tile_values.shape[2]
    chunk = tile // 2
    piece = tile // rows
    a = lax.axis_index("aa")

    route = []
    for i in range(rows):
        for j in range(cols):
            ta, tb = served_by(i, j)
            route.append((i * cols + j, ta * cols + tb))
    got = lax.ppermute(pick(tile_cols, tile_values, rows), BOTH, route)

    low = coefficients.astype(jnp.bfloat16)
    near = lax.ppermute(low, "ba", [(j, (j + 1) % cols if j % 2 else (j - 1) % cols) for j in range(cols)])
    far = lax.ppermute(low, "ba", [(j, (j - 2) % cols if j % 2 else (j + 2) % cols) for j in range(cols)])
    from_above = lax.ppermute(low, "aa", [(i, (i - 1) % rows) for i in range(rows)])
    from_below = lax.ppermute(low, "aa", [(i, (i + 1) % rows) for i in range(rows)])

    my_x, my_y, my_core = a // 4, (a // 2) % 2, a % 2
    other_y = lax.ppermute(got, "aa", [(i, i ^ 2) for i in range(rows)])
    pair = jnp.zeros((3, 2, piece, chunk), jnp.bfloat16)
    pair = lax.dynamic_update_slice(pair, got[:, None], (0, my_y, 0, 0))
    pair = lax.dynamic_update_slice(pair, other_y[:, None], (0, 1 - my_y, 0, 0))
    quad = jnp.zeros((3, 4, 2, piece, chunk), jnp.bfloat16)
    quad = lax.dynamic_update_slice(quad, pair[:, None], (0, my_x, 0, 0, 0))
    for step in (2, 1, 3):
        moved = lax.ppermute(pair, "aa", [(i, (i - 4 * step) % rows) for i in range(rows)])
        quad = lax.dynamic_update_slice(quad, moved[:, None], (0, (my_x + step) % 4, 0, 0, 0))
    quad = quad.reshape(3, 8 * piece, chunk)
    other_core = lax.ppermute(quad, "aa", [(i, i ^ 1) for i in range(rows)])
    weight = jnp.zeros((3, 2, 8 * piece, chunk), jnp.bfloat16)
    weight = lax.dynamic_update_slice(weight, quad[:, None], (0, my_core, 0, 0))
    weight = lax.dynamic_update_slice(weight, other_core[:, None], (0, 1 - my_core, 0, 0))
    weight = weight.reshape(3, tile, chunk)

    def times(left, right):
        return lax.dot_general(left, right, (((1,), (1,)), ((), ())), preferred_element_type=jnp.float32)

    def beta_part(rows_of):
        total = times(near, weight[0, rows_of])
        total = total + times(far, weight[1, rows_of])
        return total + times(low, weight[2, rows_of])

    sent = beta_part(slice(chunk, None)).astype(jnp.bfloat16)
    received = lax.ppermute(sent, "ba", [(j, j ^ 1) for j in range(cols)])
    kept = beta_part(slice(0, chunk))

    slots = jnp.arange(3, dtype=jnp.int32)

    def tile_of(block):
        slot = jnp.sum(jnp.where(tile_cols[0] == block, slots, 0))
        return lax.dynamic_slice(tile_values, (0, slot, 0, 0), (1, 1, tile, tile))[0, 0]

    alpha = jnp.dot(tile_of(a), low, preferred_element_type=jnp.float32)
    alpha = alpha + jnp.dot(tile_of((a + 1) % rows), from_above, preferred_element_type=jnp.float32)
    alpha = alpha + jnp.dot(tile_of((a + rows - 1) % rows), from_below, preferred_element_type=jnp.float32)
    energy = alpha_energy[:, None] + beta_energy[None, :]
    return alpha + energy * coefficients + kept + received.astype(jnp.float32)


def solution(mesh):
    in_specs = (P("aa", "ba"), P("aa", None, None, None), P("aa", None), P("aa"), P("ba"))
    out_specs = P("aa", "ba")
    return jax.shard_map(body, mesh=mesh, in_specs=in_specs, out_specs=out_specs, check_vma=False)
```

```python
import jax
import jax.numpy as jnp
from jax import lax
from jax.experimental import pallas as pl
from jax.experimental.pallas import tpu as pltpu
from jax.sharding import PartitionSpec as P


BOTH = ("aa", "ba")
ANY = pl.BlockSpec(memory_space=pl.ANY)
SCALARS = pl.BlockSpec(memory_space=pltpu.SMEM)
SMALL = pltpu.CompilerParams(vmem_limit_bytes=4 * 1024 * 1024)


def pick(tile_cols, tile_values):
    rows = lax.axis_size("aa")
    tile = tile_values.shape[2]
    chunk, quarter = tile // 2, tile // 4

    def kernel(cols_ref, tiles_ref, own_ref, other_ref, sems):
        row = lax.axis_index("aa")
        half = lax.rem(lax.axis_index("ba"), 2)
        core = lax.rem(row, 2)

        def copy(out_ref, core_of, t):
            place = jnp.where(half == 1, 5 - t, t)
            block = lax.rem(row + lax.div(place, 2) + rows - 1, rows)
            slot = jnp.where(cols_ref[0, 1] == block, 1, jnp.where(cols_ref[0, 2] == block, 2, 0))
            start = pl.multiple_of(half * chunk + core_of * quarter, 64)
            side = pl.multiple_of(lax.rem(place, 2) * chunk, 128)
            source = tiles_ref.at[0, slot, pl.ds(start, quarter), pl.ds(side, chunk)]
            return pltpu.make_async_copy(source, out_ref.at[t], sems.at[t + (6 if out_ref is other_ref else 0)])

        copies = [copy(other_ref, 1 - core, t) for t in range(6)] + [copy(own_ref, core, t) for t in range(6)]
        for each in copies:
            each.start()
        for each in copies:
            each.wait()

    shape = jax.ShapeDtypeStruct((6, quarter, chunk), jnp.bfloat16)
    return pl.pallas_call(
        kernel,
        out_shape=(shape, shape),
        in_specs=[SCALARS, ANY],
        out_specs=(ANY, ANY),
        scratch_shapes=[pltpu.SemaphoreType.DMA((12,))],
        compiler_params=SMALL,
        name="pick",
    )(tile_cols, tile_values)


def arrange(mine, theirs):
    count, parts, piece, chunk = mine.shape

    def kernel(mine_ref, theirs_ref, out_ref, sems):
        place = lax.axis_index("aa")
        x, core = lax.div(place, 4), lax.rem(place, 2)
        copies = []
        for index, (source, core_of) in enumerate(((mine_ref, core), (theirs_ref, 1 - core))):
            for step in range(count):
                at = pl.multiple_of(core_of * count * piece + lax.rem(x + step, count) * piece, 16)
                target = out_ref.at[:, pl.ds(at, piece), :]
                copies.append(pltpu.make_async_copy(source.at[step], target, sems.at[index * count + step]))
        for each in copies:
            each.start()
        for each in copies:
            each.wait()

    return pl.pallas_call(
        kernel,
        out_shape=jax.ShapeDtypeStruct((parts, 2 * count * piece, chunk), jnp.bfloat16),
        in_specs=[ANY, ANY],
        out_specs=ANY,
        scratch_shapes=[pltpu.SemaphoreType.DMA((2 * count,))],
        compiler_params=SMALL,
        name="arrange",
    )(mine, theirs)


def times(left, right):
    return lax.dot_general(left, right, (((1,), (1,)), ((), ())), preferred_element_type=jnp.float32)


def spread_pairs(step, cols):
    pairs = []
    for b in range(cols):
        row, upper, depth = b // 2, b // 16, b % 16
        for core in range(2):
            for y in range(2):
                x_of, y_of = row // 4, (row // 2) % 2
                source_upper = upper if y == y_of else 1 - upper
                source = (x_of * 4 + y_of * 2 + core) * cols + source_upper * 16 + depth
                target = (((x_of + step) % 4) * 4 + y * 2 + core) * cols + b
                pairs.append((source, target))
    return pairs


def body(coefficients, tile_values, tile_cols, alpha_energy, beta_energy):
    rows, cols = lax.axis_size("aa"), lax.axis_size("ba")
    tile, chunk = coefficients.shape
    a, depth = lax.axis_index("aa"), lax.axis_index("ba") % 16
    across = [(j, (j + 1) % cols if j % 2 else (j - 1) % cols) for j in range(cols)]
    within = [(j, j ^ 1) for j in range(cols)]

    low = coefficients.astype(jnp.bfloat16)
    near = lax.ppermute(low, "ba", across)
    sibling = lax.ppermute(low, "ba", within)

    own_half, other_half = pick(tile_cols, tile_values)
    holders = [
        (i * cols + j, (i ^ 1) * cols + j) for i in range(rows) for j in range(cols) if i % 8 == (j % 16) // 2
    ]
    passed = lax.ppermute(other_half, BOTH, holders)
    held = jnp.where(a % 8 == depth // 2, own_half, passed).reshape(6, 4, tile // 16, chunk)
    got = 0
    for step in (2, 1, 3, 0):
        part = lax.dynamic_index_in_dim(held, ((a // 4) + step) % 4, 1, keepdims=False)
        got = got + lax.ppermute(part, BOTH, spread_pairs(step, cols))

    above = lax.ppermute(low, "aa", [(i, (i - 1) % rows) for i in range(rows)])
    below = lax.ppermute(low, "aa", [(i, (i + 1) % rows) for i in range(rows)])
    far = lax.ppermute(sibling, "ba", across)
    next_near = lax.ppermute(near, "ba", within)
    next_far = lax.ppermute(far, "ba", within)

    pieces = {0: got}
    for step in (2, 1, 3):
        pieces[step] = lax.ppermute(got, "aa", [(i, (i - 4 * step) % rows) for i in range(rows)])
    mine = jnp.stack([pieces[step] for step in range(4)])
    theirs = lax.ppermute(mine, "aa", [(i, i ^ 1) for i in range(rows)])
    weight = arrange(mine, theirs)

    slots = jnp.arange(3, dtype=jnp.int32)

    def tile_of(block):
        slot = jnp.sum(jnp.where(tile_cols[0] == block, slots, 0))
        return lax.dynamic_slice(tile_values, (0, slot, 0, 0), (1, 1, tile, tile))[0, 0]

    total = jnp.dot(tile_of(a), low, preferred_element_type=jnp.float32)
    total = total + jnp.dot(tile_of((a + 1) % rows), above, preferred_element_type=jnp.float32)
    total = total + jnp.dot(tile_of((a + rows - 1) % rows), below, preferred_element_type=jnp.float32)
    total = total + (alpha_energy[:, None] + beta_energy[None, :]) * coefficients
    for index, value in enumerate((far, near, low, sibling, next_near, next_far)):
        total = total + times(value, weight[index])
    return total


def solution(mesh):
    in_specs = (P("aa", "ba"), P("aa", None, None, None), P("aa", None), P("aa"), P("ba"))
    out_specs = P("aa", "ba")
    return jax.shard_map(body, mesh=mesh, in_specs=in_specs, out_specs=out_specs, check_vma=False)
```

```python
import jax
import jax.numpy as jnp
from jax import lax
from jax.experimental import pallas as pl
from jax.experimental.pallas import tpu as pltpu
from jax.sharding import PartitionSpec as P


BOTH = ("aa", "ba")
ANY = pl.BlockSpec(memory_space=pl.ANY)
SCALARS = pl.BlockSpec(memory_space=pltpu.SMEM)
IN_HBM = pl.BlockSpec(memory_space=pltpu.HBM)
ON_CHIP = pl.BlockSpec(memory_space=pltpu.VMEM)
SMALL = pltpu.CompilerParams(vmem_limit_bytes=4 * 1024 * 1024)
LARGE = pltpu.CompilerParams(vmem_limit_bytes=20 * 1024 * 1024)


def prepare(tile_cols, tile_values, coefficients):
    rows = lax.axis_size("aa")
    tile = tile_values.shape[2]
    chunk, piece, steps = tile // 2, tile // 16, 3

    def kernel(cols_ref, tiles_ref, full_ref, low_ref, own_ref, other_ref, sems):
        row = lax.axis_index("aa")
        half = lax.rem(lax.axis_index("ba"), 2)
        core, x = lax.rem(row, 2), lax.div(row, 4)

        def copies():
            made = []
            for index, (out_ref, core_of) in enumerate(((other_ref, 1 - core), (own_ref, core))):
                for t in range(6):
                    place = jnp.where(half == 1, 5 - t, t)
                    block = lax.rem(row + lax.div(place, 2) + rows - 1, rows)
                    slot = jnp.where(cols_ref[0, 1] == block, 1, jnp.where(cols_ref[0, 2] == block, 2, 0))
                    side = pl.multiple_of(lax.rem(place, 2) * chunk, 128)
                    for step in range(4):
                        start = half * chunk + (core_of * 4 + lax.rem(x + step, 4)) * piece
                        source = tiles_ref.at[0, slot, pl.ds(pl.multiple_of(start, 16), piece), pl.ds(side, chunk)]
                        sem = sems.at[index * 24 + t * 4 + step]
                        made.append(pltpu.make_async_copy(source, out_ref.at[step, t], sem))
            return made

        @pl.when(pl.program_id(0) == 0)
        def _():
            for each in copies():
                each.start()

        low_ref[...] = full_ref[...].astype(jnp.bfloat16)

        @pl.when(pl.program_id(0) == steps - 1)
        def _():
            for each in copies():
                each.wait()

    shape = jax.ShapeDtypeStruct((4, 6, piece, chunk), jnp.bfloat16)
    block = pl.BlockSpec((tile // steps, chunk), lambda i: (i, 0))
    whole = pl.BlockSpec((4, 6, piece, chunk), lambda i: (0, 0, 0, 0))
    return pl.pallas_call(
        kernel,
        grid=(steps,),
        out_shape=(jax.ShapeDtypeStruct(coefficients.shape, jnp.bfloat16), shape, shape),
        in_specs=[SCALARS, IN_HBM, block],
        out_specs=(block, whole, whole),
        scratch_shapes=[pltpu.SemaphoreType.DMA((48,))],
        name="prepare",
    )(tile_cols, tile_values, coefficients)


def stack(*values):
    counts = [value.shape[0] if value.ndim == 4 else 1 for value in values]

    def kernel(*refs):
        out_ref, sems = refs[-2:]
        copies, at = [], 0
        for index, (ref, count) in enumerate(zip(refs, counts)):
            target = out_ref.at[pl.ds(at, count)] if len(ref.shape) == 4 else out_ref.at[at]
            copies.append(pltpu.make_async_copy(ref, target, sems.at[index]))
            at += count
        for each in copies:
            each.start()
        for each in copies:
            each.wait()

    return pl.pallas_call(
        kernel,
        out_shape=jax.ShapeDtypeStruct((sum(counts),) + values[0].shape[-3:], values[0].dtype),
        in_specs=[ANY] * len(values),
        out_specs=ANY,
        scratch_shapes=[pltpu.SemaphoreType.DMA((len(values),))],
        compiler_params=SMALL,
        name="stack",
    )(*values)


def choose(values):
    def kernel(*refs):
        out_ref, sem = refs[-2:]
        holder_x = lax.div(lax.axis_index("ba"), 8)
        step = lax.rem(lax.div(lax.axis_index("aa"), 4) + 4 - holder_x, 4)
        for index, ref in enumerate(refs[:-2]):

            @pl.when(step == index)
            def _():
                copy = pltpu.make_async_copy(ref, out_ref, sem)
                copy.start()
                copy.wait()

    return pl.pallas_call(
        kernel,
        out_shape=jax.ShapeDtypeStruct(values[0].shape, values[0].dtype),
        in_specs=[ANY] * len(values),
        out_specs=ANY,
        scratch_shapes=[pltpu.SemaphoreType.DMA],
        compiler_params=SMALL,
        name="choose",
    )(*values)


def alpha_part(tile_cols, tile_values, low, outer, swap, coefficients, alpha_energy, beta_energy):
    rows = lax.axis_size("aa")
    tile, chunk = low.shape

    def kernel(
        cols_ref, tiles_ref, low_ref, outer_ref, swap_ref, full_ref, alpha_ref, beta_ref, out_ref,
        rows_ref, value_ref, held_ref, sems, value_sems, held_sem,
    ):
        row = lax.axis_index("aa")
        odd = lax.rem(row, 2)
        loads = []
        for index, (shift_by, ref) in enumerate(((0, low_ref), (odd, outer_ref), (1 - odd, swap_ref))):
            block = lax.rem(row + (rows - 1 + 2 * shift_by if index else 0), rows)
            slot = jnp.where(cols_ref[0, 1] == block, 1, jnp.where(cols_ref[0, 2] == block, 2, 0))
            loads.append((
                pltpu.make_async_copy(ref, value_ref.at[pl.ds(index * tile, tile)], value_sems.at[index]),
                pltpu.make_async_copy(tiles_ref.at[0, slot], rows_ref.at[:, pl.ds(index * tile, tile)], sems.at[index]),
            ))
        last = pltpu.make_async_copy(full_ref, held_ref, held_sem)
        for pair in loads:
            for each in pair:
                each.start()
        last.start()
        for pair in loads:
            for each in pair:
                each.wait()
        last.wait()
        energy = (alpha_ref[...] + beta_ref[...]) * held_ref[...]
        out_ref[...] = energy + jnp.dot(rows_ref[...], value_ref[...], preferred_element_type=jnp.float32)

    return pl.pallas_call(
        kernel,
        out_shape=jax.ShapeDtypeStruct((tile, chunk), jnp.float32),
        in_specs=[SCALARS, IN_HBM, ANY, ANY, ANY, IN_HBM, ON_CHIP, ON_CHIP],
        out_specs=ON_CHIP,
        scratch_shapes=[
            pltpu.VMEM((tile, 3 * tile), jnp.bfloat16),
            pltpu.VMEM((3 * tile, chunk), jnp.bfloat16),
            pltpu.VMEM((tile, chunk), jnp.float32),
            pltpu.SemaphoreType.DMA((3,)),
            pltpu.SemaphoreType.DMA((3,)),
            pltpu.SemaphoreType.DMA,
        ],
        compiler_params=LARGE,
        name="alpha_part",
    )(tile_cols, tile_values, low, outer, swap, coefficients, alpha_energy[:, None], beta_energy[None, :])


def beta_part(total, mine, theirs, values):
    tile, chunk = total.shape
    count, parts, piece, _ = mine.shape
    known = len(values)

    def kernel(*refs):
        total_ref, mine_ref, theirs_ref = refs[:3]
        value_refs = refs[3 : 3 + known]
        out_ref, last_ref, weight_ref, value_ref, sems, value_sems, last_sem = refs[3 + known :]
        place = lax.axis_index("aa")
        x, core = lax.div(place, 4), lax.rem(place, 2)
        swapped = x + 1 - 2 * lax.rem(x, 2)
        copies = []
        for index, (source, core_of) in enumerate(((mine_ref, core), (theirs_ref, 1 - core))):
            for step, x_of in enumerate((x, swapped, 3 - x, 3 - swapped)):
                at = pl.multiple_of((core_of * count + x_of) * piece, 16)
                for t in range(parts):
                    target = weight_ref.at[pl.ds(at, piece), pl.ds(t * chunk, chunk)]
                    sem = sems.at[(index * count + step) * parts + t]
                    copies.append(pltpu.make_async_copy(source.at[step, t], target, sem))
        for index, ref in enumerate(value_refs):
            target = value_ref.at[:, pl.ds(index * chunk, chunk)]
            copies.append(pltpu.make_async_copy(ref, target, value_sems.at[index]))
        for each in copies:
            each.start()
        for each in copies:
            each.wait()
        last = pltpu.make_async_copy(weight_ref.at[:, pl.ds(known * chunk, chunk)], last_ref, last_sem)
        last.start()
        out_ref[...] = total_ref[...] + times(value_ref[...], weight_ref[:, : known * chunk])
        last.wait()

    return pl.pallas_call(
        kernel,
        out_shape=(
            jax.ShapeDtypeStruct((tile, chunk), jnp.float32),
            jax.ShapeDtypeStruct((chunk, chunk), jnp.bfloat16),
        ),
        in_specs=[ON_CHIP, ANY, ANY] + [ANY] * known,
        out_specs=(ON_CHIP, ANY),
        scratch_shapes=[
            pltpu.VMEM((chunk, parts * chunk), jnp.bfloat16),
            pltpu.VMEM((tile, known * chunk), jnp.bfloat16),
            pltpu.SemaphoreType.DMA((2 * count * parts,)),
            pltpu.SemaphoreType.DMA((known,)),
            pltpu.SemaphoreType.DMA,
        ],
        compiler_params=LARGE,
        name="beta_part",
    )(total, mine, theirs, *values)


def times(left, right):
    return lax.dot_general(left, right, (((1,), (1,)), ((), ())), preferred_element_type=jnp.float32)


def spread_pairs(step, cols):
    pairs = []
    for b in range(cols):
        row, upper, depth = b // 2, b // 16, b % 16
        for core in range(2):
            for y in range(2):
                x_of, y_of = row // 4, (row // 2) % 2
                source_upper = upper if y == y_of else 1 - upper
                source = (x_of * 4 + y_of * 2 + core) * cols + source_upper * 16 + depth
                target = (((x_of + step) % 4) * 4 + y * 2 + core) * cols + b
                pairs.append((source, target))
    return pairs


def body(coefficients, tile_values, tile_cols, alpha_energy, beta_energy):
    rows, cols = lax.axis_size("aa"), lax.axis_size("ba")
    a, depth = lax.axis_index("aa"), lax.axis_index("ba") % 16
    across = [(j, (j + 1) % cols if j % 2 else (j - 1) % cols) for j in range(cols)]
    within = [(j, j ^ 1) for j in range(cols)]

    low, own_half, other_half = prepare(tile_cols, tile_values, coefficients)
    near = lax.ppermute(low, "ba", across)
    sibling = lax.ppermute(low, "ba", within)

    holders = [
        (i * cols + j, (i ^ 1) * cols + j) for i in range(rows) for j in range(cols) if i % 8 == (j % 16) // 2
    ]
    passed = lax.ppermute(other_half, BOTH, holders)
    held = jnp.where(a % 8 == depth // 2, own_half, passed)
    spread = [lax.ppermute(held[step], BOTH, spread_pairs(step, cols)) for step in range(4)]
    got = choose(spread)

    outer = lax.ppermute(low, "aa", [(i, (i + 1) % rows if i % 2 else (i - 1) % rows) for i in range(rows)])
    swap = lax.ppermute(low, "aa", [(i, i ^ 1) for i in range(rows)])
    far = lax.ppermute(sibling, "ba", across)
    next_near = lax.ppermute(near, "ba", within)
    next_far = lax.ppermute(far, "ba", within)

    pair = stack(got, lax.ppermute(got, "aa", [(i, i ^ 4) for i in range(rows)]))
    mine = stack(pair, lax.ppermute(pair, "aa", [(i, i ^ 12) for i in range(rows)]))
    theirs = lax.ppermute(mine, "aa", [(i, i ^ 1) for i in range(rows)])

    total = alpha_part(tile_cols, tile_values, low, outer, swap, coefficients, alpha_energy, beta_energy)
    total, last = beta_part(total, mine, theirs, (far, near, low, sibling, next_near))
    return total + times(next_far, last)


def solution(mesh):
    in_specs = (P("aa", "ba"), P("aa", None, None, None), P("aa", None), P("aa"), P("ba"))
    out_specs = P("aa", "ba")
    return jax.shard_map(body, mesh=mesh, in_specs=in_specs, out_specs=out_specs, check_vma=False)
```

```python
import jax
import jax.numpy as jnp
from jax import lax
from jax.experimental import pallas as pl
from jax.experimental.pallas import tpu as pltpu
from jax.sharding import PartitionSpec as P


BOTH = ("aa", "ba")
ANY = pl.BlockSpec(memory_space=pl.ANY)
SCALARS = pl.BlockSpec(memory_space=pltpu.SMEM)
IN_HBM = pl.BlockSpec(memory_space=pltpu.HBM)
ON_CHIP = pl.BlockSpec(memory_space=pltpu.VMEM)
SMALL = pltpu.CompilerParams(vmem_limit_bytes=4 * 1024 * 1024)
LARGE = pltpu.CompilerParams(vmem_limit_bytes=20 * 1024 * 1024)


def prepare(tile_cols, tile_values, coefficients):
    rows = lax.axis_size("aa")
    tile = tile_values.shape[2]
    chunk, piece, steps = tile // 2, tile // 16, 3

    def kernel(cols_ref, tiles_ref, full_ref, low_ref, own_ref, other_ref, sems):
        row = lax.axis_index("aa")
        half = lax.rem(lax.axis_index("ba"), 2)
        core, x = lax.rem(row, 2), lax.div(row, 4)

        def copies():
            made = []
            for index, (out_ref, core_of) in enumerate(((other_ref, 1 - core), (own_ref, core))):
                for t in range(6):
                    place = jnp.where(half == 1, 5 - t, t)
                    block = lax.rem(row + lax.div(place, 2) + rows - 1, rows)
                    slot = jnp.where(cols_ref[0, 1] == block, 1, jnp.where(cols_ref[0, 2] == block, 2, 0))
                    side = pl.multiple_of(lax.rem(place, 2) * chunk, 128)
                    for step in range(4):
                        start = half * chunk + (core_of * 4 + lax.rem(x + step, 4)) * piece
                        source = tiles_ref.at[0, slot, pl.ds(pl.multiple_of(start, 16), piece), pl.ds(side, chunk)]
                        sem = sems.at[index * 24 + t * 4 + step]
                        made.append(pltpu.make_async_copy(source, out_ref.at[step, t], sem))
            return made

        holds = lax.rem(row, 8) == lax.div(lax.rem(lax.axis_index("ba"), 16), 2)

        @pl.when(holds & (pl.program_id(0) == 0))
        def _():
            for each in copies():
                each.start()

        low_ref[...] = full_ref[...].astype(jnp.bfloat16)

        @pl.when(holds & (pl.program_id(0) == steps - 1))
        def _():
            for each in copies():
                each.wait()

    shape = jax.ShapeDtypeStruct((4, 6, piece, chunk), jnp.bfloat16)
    block = pl.BlockSpec((tile // steps, chunk), lambda i: (i, 0))
    whole = pl.BlockSpec((4, 6, piece, chunk), lambda i: (0, 0, 0, 0))
    return pl.pallas_call(
        kernel,
        grid=(steps,),
        out_shape=(jax.ShapeDtypeStruct(coefficients.shape, jnp.bfloat16), shape, shape),
        in_specs=[SCALARS, IN_HBM, block],
        out_specs=(block, whole, whole),
        scratch_shapes=[pltpu.SemaphoreType.DMA((48,))],
        name="prepare",
    )(tile_cols, tile_values, coefficients)


def stack(*values):
    counts = [value.shape[0] if value.ndim == 4 else 1 for value in values]

    def kernel(*refs):
        out_ref, sems = refs[-2:]
        copies, at = [], 0
        for index, (ref, count) in enumerate(zip(refs, counts)):
            target = out_ref.at[pl.ds(at, count)] if len(ref.shape) == 4 else out_ref.at[at]
            copies.append(pltpu.make_async_copy(ref, target, sems.at[index]))
            at += count
        for each in copies:
            each.start()
        for each in copies:
            each.wait()

    return pl.pallas_call(
        kernel,
        out_shape=jax.ShapeDtypeStruct((sum(counts),) + values[0].shape[-3:], values[0].dtype),
        in_specs=[ANY] * len(values),
        out_specs=ANY,
        scratch_shapes=[pltpu.SemaphoreType.DMA((len(values),))],
        compiler_params=SMALL,
        name="stack",
    )(*values)


def choose(values):
    def kernel(*refs):
        out_ref, sem = refs[-2:]
        holder_x = lax.div(lax.axis_index("ba"), 8)
        step = lax.rem(lax.div(lax.axis_index("aa"), 4) + 4 - holder_x, 4)
        for index, ref in enumerate(refs[:-2]):

            @pl.when(step == index)
            def _():
                copy = pltpu.make_async_copy(ref, out_ref, sem)
                copy.start()
                copy.wait()

    return pl.pallas_call(
        kernel,
        out_shape=jax.ShapeDtypeStruct(values[0].shape, values[0].dtype),
        in_specs=[ANY] * len(values),
        out_specs=ANY,
        scratch_shapes=[pltpu.SemaphoreType.DMA],
        compiler_params=SMALL,
        name="choose",
    )(*values)


def alpha_part(tile_cols, tile_values, low, outer, swap, coefficients, alpha_energy, beta_energy):
    rows = lax.axis_size("aa")
    tile, chunk = low.shape

    def kernel(
        cols_ref, tiles_ref, low_ref, outer_ref, swap_ref, full_ref, alpha_ref, beta_ref, out_ref,
        rows_ref, value_ref, held_ref, sems, value_sems, held_sem,
    ):
        row = lax.axis_index("aa")
        odd = lax.rem(row, 2)
        loads = []
        for index, (shift_by, ref) in enumerate(((0, low_ref), (odd, outer_ref), (1 - odd, swap_ref))):
            block = lax.rem(row + (rows - 1 + 2 * shift_by if index else 0), rows)
            slot = jnp.where(cols_ref[0, 1] == block, 1, jnp.where(cols_ref[0, 2] == block, 2, 0))
            loads.append((
                pltpu.make_async_copy(ref, value_ref.at[pl.ds(index * tile, tile)], value_sems.at[index]),
                pltpu.make_async_copy(tiles_ref.at[0, slot], rows_ref.at[:, pl.ds(index * tile, tile)], sems.at[index]),
            ))
        last = pltpu.make_async_copy(full_ref, held_ref, held_sem)
        for pair in loads:
            for each in pair:
                each.start()
        last.start()
        for pair in loads:
            for each in pair:
                each.wait()
        last.wait()
        energy = (alpha_ref[...] + beta_ref[...]) * held_ref[...]
        out_ref[...] = energy + jnp.dot(rows_ref[...], value_ref[...], preferred_element_type=jnp.float32)

    return pl.pallas_call(
        kernel,
        out_shape=jax.ShapeDtypeStruct((tile, chunk), jnp.float32),
        in_specs=[SCALARS, IN_HBM, ANY, ANY, ANY, IN_HBM, ON_CHIP, ON_CHIP],
        out_specs=ON_CHIP,
        scratch_shapes=[
            pltpu.VMEM((tile, 3 * tile), jnp.bfloat16),
            pltpu.VMEM((3 * tile, chunk), jnp.bfloat16),
            pltpu.VMEM((tile, chunk), jnp.float32),
            pltpu.SemaphoreType.DMA((3,)),
            pltpu.SemaphoreType.DMA((3,)),
            pltpu.SemaphoreType.DMA,
        ],
        compiler_params=LARGE,
        name="alpha_part",
    )(tile_cols, tile_values, low, outer, swap, coefficients, alpha_energy[:, None], beta_energy[None, :])


def beta_part(total, mine, theirs, values):
    tile, chunk = total.shape
    count, parts, piece, _ = mine.shape
    known = len(values)

    def kernel(*refs):
        total_ref, mine_ref, theirs_ref = refs[:3]
        value_refs = refs[3 : 3 + known]
        out_ref, last_ref, weight_ref, value_ref, sems, value_sems, last_sem = refs[3 + known :]
        place = lax.axis_index("aa")
        x, core = lax.div(place, 4), lax.rem(place, 2)
        swapped = x + 1 - 2 * lax.rem(x, 2)
        copies = []
        for index, (source, core_of) in enumerate(((mine_ref, core), (theirs_ref, 1 - core))):
            for step, x_of in enumerate((x, swapped, 3 - x, 3 - swapped)):
                at = pl.multiple_of((core_of * count + x_of) * piece, 16)
                for t in range(parts):
                    target = weight_ref.at[pl.ds(at, piece), pl.ds(t * chunk, chunk)]
                    sem = sems.at[(index * count + step) * parts + t]
                    copies.append(pltpu.make_async_copy(source.at[step, t], target, sem))
        for index, ref in enumerate(value_refs):
            target = value_ref.at[:, pl.ds(index * chunk, chunk)]
            copies.append(pltpu.make_async_copy(ref, target, value_sems.at[index]))
        for each in copies:
            each.start()
        for each in copies:
            each.wait()
        last = pltpu.make_async_copy(weight_ref.at[:, pl.ds(known * chunk, chunk)], last_ref, last_sem)
        last.start()
        out_ref[...] = total_ref[...] + times(value_ref[...], weight_ref[:, : known * chunk])
        last.wait()

    return pl.pallas_call(
        kernel,
        out_shape=(
            jax.ShapeDtypeStruct((tile, chunk), jnp.float32),
            jax.ShapeDtypeStruct((chunk, chunk), jnp.bfloat16),
        ),
        in_specs=[ON_CHIP, ANY, ANY] + [ANY] * known,
        out_specs=(ON_CHIP, ANY),
        scratch_shapes=[
            pltpu.VMEM((chunk, parts * chunk), jnp.bfloat16),
            pltpu.VMEM((tile, known * chunk), jnp.bfloat16),
            pltpu.SemaphoreType.DMA((2 * count * parts,)),
            pltpu.SemaphoreType.DMA((known,)),
            pltpu.SemaphoreType.DMA,
        ],
        compiler_params=LARGE,
        name="beta_part",
    )(total, mine, theirs, *values)


def times(left, right):
    return lax.dot_general(left, right, (((1,), (1,)), ((), ())), preferred_element_type=jnp.float32)


def spread_pairs(step, cols):
    pairs = []
    for b in range(cols):
        row, upper, depth = b // 2, b // 16, b % 16
        for core in range(2):
            for y in range(2):
                x_of, y_of = row // 4, (row // 2) % 2
                source_upper = upper if y == y_of else 1 - upper
                source = (x_of * 4 + y_of * 2 + core) * cols + source_upper * 16 + depth
                target = (((x_of + step) % 4) * 4 + y * 2 + core) * cols + b
                pairs.append((source, target))
    return pairs


def body(coefficients, tile_values, tile_cols, alpha_energy, beta_energy):
    rows, cols = lax.axis_size("aa"), lax.axis_size("ba")
    a, depth = lax.axis_index("aa"), lax.axis_index("ba") % 16
    across = [(j, (j + 1) % cols if j % 2 else (j - 1) % cols) for j in range(cols)]
    within = [(j, j ^ 1) for j in range(cols)]

    low, own_half, other_half = prepare(tile_cols, tile_values, coefficients)
    near = lax.ppermute(low, "ba", across)
    sibling = lax.ppermute(low, "ba", within)

    holders = [
        (i * cols + j, (i ^ 1) * cols + j) for i in range(rows) for j in range(cols) if i % 8 == (j % 16) // 2
    ]
    passed = lax.ppermute(other_half, BOTH, holders)
    held = jnp.where(a % 8 == depth // 2, own_half, passed)
    spread = [lax.ppermute(held[step], BOTH, spread_pairs(step, cols)) for step in range(4)]
    got = choose(spread)

    outer = lax.ppermute(low, "aa", [(i, (i + 1) % rows if i % 2 else (i - 1) % rows) for i in range(rows)])
    swap = lax.ppermute(low, "aa", [(i, i ^ 1) for i in range(rows)])
    far = lax.ppermute(sibling, "ba", across)
    next_near = lax.ppermute(near, "ba", within)
    next_far = lax.ppermute(far, "ba", within)

    pair = stack(got, lax.ppermute(got, "aa", [(i, i ^ 4) for i in range(rows)]))
    mine = stack(pair, lax.ppermute(pair, "aa", [(i, i ^ 12) for i in range(rows)]))
    theirs = lax.ppermute(mine, "aa", [(i, i ^ 1) for i in range(rows)])

    total = alpha_part(tile_cols, tile_values, low, outer, swap, coefficients, alpha_energy, beta_energy)
    total, last = beta_part(total, mine, theirs, (far, near, low, sibling, next_near))
    return total + times(next_far, last)


def solution(mesh):
    in_specs = (P("aa", "ba"), P("aa", None, None, None), P("aa", None), P("aa"), P("ba"))
    out_specs = P("aa", "ba")
    return jax.shard_map(body, mesh=mesh, in_specs=in_specs, out_specs=out_specs, check_vma=False)
```
